32 devices in a mesh: ctx: 8 (over z, x), tp: 4 (over y, core).
Axes of the slice: x: 2, y: 2, z: 4, core: 2. Of those that a mesh axis runs over, the one named last changes fastest.
Arguments:
- query: bfloat16 [4096, 5120], P(('ctx', 'tp')), may hold values from -5 to 5
- key_in: bfloat16 [4096, 5120], P(('ctx', 'tp')), may hold values from -5 to 5
- value_in: bfloat16 [4096, 5120], P(('ctx', 'tp')), may hold values from -6 to 6
- out_grad: bfloat16 [4096, 5120], P(('ctx', 'tp')), may hold values from -18 to 18
- lengths: int32 [32], replicated, may hold values from 1 to 512, 4096 in all
Outputs:
- query_grad: bfloat16 [4096, 5120], P(('ctx', 'tp'))
- key_grad: bfloat16 [4096, 5120], P(('ctx', 'tp'))
- value_grad: bfloat16 [4096, 5120], P(('ctx', 'tp'))
The draws below stay inside these ranges and needn't reach their ends.
Inputs may be any that keep to these rules, and one draw needn't show every extreme that they name: lengths[p] is the number of residues of protein p; proteins follow one another in list order, the lengths sum to 4096, and the longest has exactly 512 residues.
All inputs are finite; a program needn't handle non-finite values.
Results may differ from the reference program's by a relative error of at most 0.019.
Values may be sent and summed in bfloat16 or wider, within the bound.
No kernel may reach another device: no remote copies, remote signals or barrier semaphores. Data moves between devices by JAX's collectives and lax.ppermute only.
A program may use at most 192 MiB of HBM per device.

```python
import math
import jax
import jax.numpy as jnp
import numpy as np
from jax import lax

HEADS = 40
HEAD_DIM = 128
TOK_DEV = 512
TOKENS = 4096
PROTEINS = 32


def draw_both(key):
    base = jax.random.fold_in(key, 7001)
    first_key, second_key, scale_key = jax.random.split(base, 3)
    width = HEADS * HEAD_DIM
    row_scale = jnp.exp(jax.random.uniform(scale_key, (TOKENS, 1), jnp.float32, jnp.log(0.3), jnp.log(3.0)))
    queries = jax.random.normal(first_key, (TOKENS, width), jnp.float32)
    keys = jax.random.normal(second_key, (TOKENS, width), jnp.float32) * row_scale
    return (jnp.clip(queries, -5.0, 5.0), jnp.clip(keys, -5.0, 5.0))


def draw_query(key, part):
    return draw_both(key)[0].astype(jnp.bfloat16)


def draw_key_in(key, part):
    return draw_both(key)[1].astype(jnp.bfloat16)


def level_of(stream_key, extent, pieces, low, largest):
    factor_of = 1.0
    for position, shards_of in pieces:
        heights = jax.random.uniform(jax.random.fold_in(jax.random.fold_in(stream_key, 6), position), (shards_of,), jnp.float32, low / len(pieces), largest / len(pieces))
        factor_of = factor_of * jnp.repeat(jnp.exp(heights), extent[position] // shards_of).reshape((-1,) + (1,) * (len(extent) - 1 - position))
    return factor_of


def length_profile(count, total, bound, lean):
    loads = [(1 << 20) // math.isqrt(grade ** lean) + 1 for grade in range(2, count + 1)]
    spare, holding = total - bound - (count - 1), [1] * (count - 1)
    while spare > 0:
        candidates = [i for i in range(count - 1) if holding[i] < bound]
        whole, remaining = sum([loads[i] for i in candidates]), spare
        for i in candidates:
            extra = min(bound - holding[i], max(1, remaining * loads[i] // whole), spare)
            holding[i] = holding[i] + extra
            spare = spare - extra
    return np.array([bound] + holding)


def uneven(own_key, number_of, total, most, slope):
    if number_of == 2:
        one = jax.random.randint(own_key, (), max(1, total - most), min(most, total - 1) + 1)
        return jnp.stack([one, total - one])
    tallies = jnp.asarray(length_profile(number_of, total, most, slope), jnp.int32)
    twos = (number_of - 1) // 2
    giver, receiver = tallies[1:1 + 2 * twos:2], tallies[2:2 + 2 * twos:2]
    slack = jnp.minimum(giver - 1, most - receiver)
    passed = jax.random.randint(jax.random.fold_in(own_key, 1), (twos,), 0, 1 << 20) % (slack + 1)
    tallies = tallies.at[1:1 + 2 * twos:2].set(giver - passed).at[2:2 + 2 * twos:2].set(receiver + passed)
    return tallies[jax.random.permutation(jax.random.fold_in(own_key, 2), number_of)]


def centred(own_key, dims, scale, limit, cuts=(), kind=jnp.bfloat16):
    drawn = jax.random.normal(own_key, dims, jnp.float32) * scale
    if len(cuts) > 0:
        drawn = level_of(own_key, dims, cuts, -0.22, 0.18) * drawn
    return jnp.clip(drawn, min=-limit, max=limit).astype(kind)


def setup_inputs(seed: int = 0) -> dict:
    key_list = jax.random.split(jax.random.key(seed), 6)
    return {
        "query": draw_query(jax.random.fold_in(key_list[5], 71), 0),
        "key_in": draw_key_in(jax.random.fold_in(key_list[5], 71), 0),
        "value_in": centred(key_list[2], (TOKENS, HEADS * HEAD_DIM), 1.0, 6.0, ((0, 32),)),
        "out_grad": centred(key_list[3], (TOKENS, HEADS * HEAD_DIM), 3.0, 18.0, ((0, 32),)),
        "lengths": uneven(key_list[4], PROTEINS, TOKENS, TOK_DEV, 2).astype(jnp.int32),
    }


NEG = -1.0e30


def segment_ids(lengths, first, count):
    bounds = jnp.cumsum(lengths).astype(jnp.int32)
    positions = (first + jnp.arange(count, dtype=jnp.int32)).astype(jnp.int32)
    inside = jnp.sum((bounds[None, :] <= positions[:, None]).astype(jnp.int32), axis=1)
    return jnp.where(positions < 0, -1, inside).astype(jnp.int32)


def reference(query, key_in, value_in, out_grad, lengths):
    rows = TOK_DEV
    width = HEADS * HEAD_DIM
    scale = HEAD_DIM ** -0.5
    seg_all = segment_ids(lengths, -rows, TOKENS + 2 * rows)
    zero_rim = jnp.zeros((rows, width), jnp.bfloat16)
    key_wide = jnp.concatenate((zero_rim, key_in, zero_rim), axis=0)
    value_wide = jnp.concatenate((zero_rim, value_in, zero_rim), axis=0)

    def split(block):
        return block.astype(jnp.float32).reshape(block.shape[0], HEADS, HEAD_DIM)

    def step(carry, number):
        key_acc, value_acc = carry
        first = (number * rows).astype(jnp.int32)
        queries = split(lax.dynamic_slice_in_dim(query, first, rows, 0))
        grads_out = split(lax.dynamic_slice_in_dim(out_grad, first, rows, 0))
        keys = split(lax.dynamic_slice_in_dim(key_wide, first, 3 * rows, 0))
        values = split(lax.dynamic_slice_in_dim(value_wide, first, 3 * rows, 0))
        seg_rows = lax.dynamic_slice_in_dim(seg_all, first + rows, rows, 0)
        seg_cols = lax.dynamic_slice_in_dim(seg_all, first, 3 * rows, 0)
        scores = jnp.einsum("qhd,khd->hqk", queries, keys) * scale
        scores = jnp.where(seg_rows[None, :, None] == seg_cols[None, None, :], scores, NEG)
        row_top = jnp.max(scores, axis=2)
        log_total = row_top + jnp.log(jnp.sum(jnp.exp(scores - row_top[:, :, None]), axis=2))
        probs = jnp.exp(scores - log_total[:, :, None])
        probs_b = lax.optimization_barrier(probs.astype(jnp.bfloat16)).astype(jnp.float32)
        attended = jnp.einsum("hqk,khd->qhd", probs_b, values)
        row_dot = jnp.einsum("qhd,qhd->hq", grads_out, attended)
        dprob = jnp.einsum("qhd,khd->hqk", grads_out, values)
        dscore = lax.optimization_barrier((probs * (dprob - row_dot[:, :, None])).astype(jnp.bfloat16)).astype(jnp.float32)
        query_term = jnp.einsum("hqk,khd->qhd", dscore, keys) * scale
        key_term = jnp.einsum("hqk,qhd->khd", dscore, queries) * scale
        value_term = jnp.einsum("hqk,qhd->khd", probs_b, grads_out)
        key_old = lax.dynamic_slice_in_dim(key_acc, first, 3 * rows, 0)
        value_old = lax.dynamic_slice_in_dim(value_acc, first, 3 * rows, 0)
        key_acc = lax.dynamic_update_slice_in_dim(key_acc, key_old + key_term.reshape(3 * rows, width), first, 0)
        value_acc = lax.dynamic_update_slice_in_dim(value_acc, value_old + value_term.reshape(3 * rows, width), first, 0)
        return (key_acc, value_acc), query_term.reshape(rows, width).astype(jnp.bfloat16)

    start_acc = jnp.zeros((TOKENS + 2 * rows, width), jnp.float32)
    carry, query_blocks = lax.scan(step, (start_acc, start_acc), jnp.arange(TOKENS // rows, dtype=jnp.int32))
    key_acc, value_acc = carry
    query_grad = query_blocks.reshape(TOKENS, width)
    key_grad = key_acc[rows:TOKENS + rows].astype(jnp.bfloat16)
    value_grad = value_acc[rows:TOKENS + rows].astype(jnp.bfloat16)
    return (query_grad, key_grad, value_grad)
```

```python
import functools

import jax
import jax.numpy as jnp
import numpy as np
from jax import lax
from jax.experimental import pallas as pl
from jax.experimental.pallas import tpu as pltpu
from jax.sharding import Mesh
from jax.sharding import PartitionSpec as P

HEAD_DIM = 128
NEG = -1e30
FLOOR = -1e29
UNIT = 128
TILE = 256
WIDTHS = (2, 3, 4, 5, 6, 8, 10)


def pack_kernel(*refs):
    ins, out = refs[:-1], refs[-1]
    for number, ref in enumerate(ins):
        out[0, number] = ref[...]


def pack(arrays, peers, first, count):
    rows, width = arrays[0].shape
    each = width // peers
    spec = pl.BlockSpec(
        (pl.Element(rows), pl.Element(count)), lambda d: (0, pl.multiple_of(d * each + first, 128))
    )
    return pl.pallas_call(
        pack_kernel,
        grid=(peers,),
        in_specs=[spec] * len(arrays),
        out_specs=pl.BlockSpec((1, len(arrays), rows, count), lambda d: (d, 0, 0, 0)),
        out_shape=jax.ShapeDtypeStruct((peers, len(arrays), rows, count), arrays[0].dtype),
        name="pack",
    )(*arrays)


def unpack_kernel(spans, kinds, *refs):
    ins, outs = refs[: len(spans)], refs[len(spans) :]
    for (first, count), ref in zip(spans, ins):
        for kind in range(kinds):
            outs[kind][:, first : first + count] = ref[0, kind]


def unpack(blocks, spans):
    peers, kinds, rows, _ = blocks[0].shape
    each = sum(count for _, count in spans)
    return pl.pallas_call(
        functools.partial(unpack_kernel, spans, kinds),
        grid=(peers,),
        in_specs=[
            pl.BlockSpec((1, kinds, rows, count), lambda d: (d, 0, 0, 0)) for _, count in spans
        ],
        out_specs=[pl.BlockSpec((rows, each), lambda d: (0, d))] * kinds,
        out_shape=[jax.ShapeDtypeStruct((rows, peers * each), blocks[0].dtype)] * kinds,
        name="unpack",
    )(*blocks)


def attention_kernel(
    widths,
    half,
    meta,
    seg_key,
    seg_query,
    left,
    own,
    right,
    out_left,
    out_own,
    out_right,
    qw,
    kw,
    vw,
    gw,
    kt,
    dq,
    dk,
    dv,
):
    window = qw.shape[0]
    scale = HEAD_DIM ** (-0.5)
    factor = scale * float(np.log2(np.e))
    group = window - 2 * half
    parts = ((left, 0, half), (own, half, group), (right, half + group, half))
    for number, target in enumerate((qw, kw, vw, gw)):
        for source, first, count in parts:
            target[first : first + count] = source[:, number].reshape(count, HEAD_DIM)
    for tile in range(window // TILE):
        kt[:, tile * TILE : (tile + 1) * TILE] = kw[tile * TILE : (tile + 1) * TILE].T
    dq[...] = jnp.zeros_like(dq)
    dk[...] = jnp.zeros_like(dk)
    dv[...] = jnp.zeros_like(dv)

    def visit(tile, width):
        rows = pl.ds(pl.multiple_of(tile * TILE, TILE), TILE)
        keys = pl.ds(pl.multiple_of(meta[0, tile] * UNIT, UNIT), width * UNIT)
        q, g, k, v = qw[rows], gw[rows], kw[keys], vw[keys]
        over = (((1,), (1,)), ((), ()))
        scores = lax.dot_general(k, q, over, preferred_element_type=jnp.float32)
        dprob = lax.dot_general(v, g, over, preferred_element_type=jnp.float32)
        marks = jnp.concatenate([seg_key[keys]] * (TILE // 128), axis=1)
        scores = jnp.where(marks == seg_query[:, rows], scores, NEG)
        top = jnp.maximum(jnp.max(scores, axis=0, keepdims=True), FLOOR)
        raised = jnp.exp2((scores - top) * factor)
        total = jnp.sum(raised, axis=0, keepdims=True)
        inverse = jnp.where(total > 0.0, 1.0 / total, 0.0)
        dot = jnp.sum(raised * dprob, axis=0, keepdims=True) * inverse
        probs = raised * inverse
        probs_b = probs.astype(jnp.bfloat16)
        dscore = (probs * (dprob - dot)).astype(jnp.bfloat16)
        dv[keys] += jnp.dot(probs_b, g, preferred_element_type=jnp.float32)
        dk[keys] += jnp.dot(dscore, q, preferred_element_type=jnp.float32)
        turned = jnp.dot(kt[:, keys], dscore, preferred_element_type=jnp.float32)
        dq[rows] = turned.T * scale

    def step(tile, carry):
        for width in widths:
            pl.when(meta[1, tile] == width)(functools.partial(visit, tile, width))
        return carry

    lax.fori_loop(0, window // TILE, step, 0)
    for target, first, count in (
        (out_left, 0, half),
        (out_own, half, group),
        (out_right, half + group, half),
    ):
        shape = (target.shape[0],) + target.shape[2:]
        span = slice(first, first + count)
        target[:, 0] = dq[span].astype(jnp.bfloat16).reshape(shape)
        target[:, 1] = (dk[span] * scale).astype(jnp.bfloat16).reshape(shape)
        target[:, 2] = dv[span].astype(jnp.bfloat16).reshape(shape)


def attention(meta, seg_key, seg_query, left, own, right, widths):
    peers, kinds, rows, width = own.shape
    edge = left.shape[0]
    half = edge * rows
    window = peers * rows + 2 * half

    def block(count, number):
        return pl.BlockSpec((count, number, rows, HEAD_DIM), lambda h, _: (0, 0, 0, h))

    def shape(count):
        return jax.ShapeDtypeStruct((count, 3, rows, width), jnp.bfloat16)

    elements = width // HEAD_DIM * window * 5 * UNIT
    return pl.pallas_call(
        functools.partial(attention_kernel, widths, half),
        grid_spec=pltpu.PrefetchScalarGridSpec(
            num_scalar_prefetch=1,
            grid=(width // HEAD_DIM,),
            in_specs=[
                pl.BlockSpec((window, 128), lambda h, _: (0, 0)),
                pl.BlockSpec((1, window), lambda h, _: (0, 0)),
                block(edge, 4),
                block(peers, 4),
                block(edge, 4),
            ],
            out_specs=[block(edge, 3), block(peers, 3), block(edge, 3)],
            scratch_shapes=[pltpu.VMEM((window, HEAD_DIM), jnp.bfloat16)] * 4
            + [pltpu.VMEM((HEAD_DIM, window), jnp.bfloat16)]
            + [pltpu.VMEM((window, HEAD_DIM), jnp.float32)] * 3,
        ),
        out_shape=[shape(edge), shape(peers), shape(edge)],
        cost_estimate=pl.CostEstimate(
            flops=elements * 10 * HEAD_DIM,
            transcendentals=elements,
            bytes_accessed=own.size * 4 + left.size * 8,
        ),
        name="attention",
    )(meta, seg_key, seg_query, left, own, right)


def plan(lengths, me, group, half, tokens, widths):
    window = group + 2 * half
    count = lengths.shape[0]
    order = jnp.arange(count, dtype=jnp.int32)
    ends = jnp.sum(jnp.where(order[:, None] <= order[None, :], lengths[:, None], 0), axis=0)
    base = me * group - half
    at = base + jnp.arange(window, dtype=jnp.int32)
    passed = ends[:, None] <= at[None, :]
    seg = jnp.sum(passed.astype(jnp.int32), axis=0)
    start = jnp.sum(jnp.where(passed, lengths[:, None], 0), axis=0)
    end = jnp.min(jnp.where(passed, tokens, ends[:, None]), axis=0)
    low, high = start // group, (end - 1) // group
    edge = high * group
    owner = jnp.where((low == high) | (edge - start >= end - edge), low, high)
    valid = (owner == me) & (at >= 0) & (at < tokens)
    seg_key = jnp.broadcast_to(jnp.where(valid, seg, -1)[:, None], (window, 128))
    seg_query = jnp.where(valid, seg, -2)[None, :]
    first = jnp.min(jnp.where(valid, start - base, window).reshape(-1, TILE), axis=1) // UNIT
    last = jnp.max(jnp.where(valid, end - base, 0).reshape(-1, TILE), axis=1)
    need = (last + UNIT - 1) // UNIT - first
    chosen = jnp.full_like(need, widths[-1])
    for width in reversed(widths):
        chosen = jnp.where(need <= width, width, chosen)
    chosen = jnp.where(last > 0, chosen, 0)
    first = jnp.clip(first, 0, window // UNIT - chosen)
    return jnp.stack([first, chosen]).astype(jnp.int32), seg_key, seg_query


def shards(query, key_in, value_in, out_grad, lengths):
    arrays = (query, key_in, value_in, out_grad)
    plane = ("r", "tp")
    groups = lax.axis_size("g")
    peers = lax.axis_size("r") * lax.axis_size("tp")
    rows, width = query.shape
    each = width // peers
    group = rows * peers
    half = rows * lax.axis_size("tp") // 2
    edge = half // rows
    window = group + 2 * half
    tokens = group * groups
    widths = tuple(w for w in WIDTHS if w < window // UNIT and w <= 10)
    if window // UNIT <= 10:
        widths = widths + (window // UNIT,)
    meta, seg_key, seg_query = plan(lengths, lax.axis_index("g"), group, half, tokens, widths)
    up = [(i, i + 1) for i in range(groups - 1)]
    down = [(i + 1, i) for i in range(groups - 1)]
    heads = each // HEAD_DIM
    counts = (heads - heads // 2, heads // 2)
    spans, first = [], 0
    for count in counts:
        if count:
            spans.append((first * HEAD_DIM, count * HEAD_DIM))
            first += count
    gathered = []
    for first, count in spans:
        packed = pack(arrays, peers, first, count)
        own = lax.all_to_all(packed, plane, split_axis=0, concat_axis=0, tiled=True)
        gathered.append(own)
    returned = []
    for own in gathered:
        left = lax.ppermute(own[peers - edge :], "g", up)
        right = lax.ppermute(own[:edge], "g", down)
        out_left, out_own, out_right = attention(
            meta, seg_key, seg_query, left, own, right, widths
        )
        from_right = lax.ppermute(out_left, "g", down)
        from_left = lax.ppermute(out_right, "g", up)
        out_own = out_own.at[:edge].add(from_left)
        out_own = out_own.at[peers - edge :].add(from_right)
        returned.append(
            lax.all_to_all(out_own, plane, split_axis=0, concat_axis=0, tiled=True)
        )
    return tuple(unpack(returned, spans))


def solution(mesh):
    ctx, tp = mesh.devices.shape
    heads_of = lambda width: width // HEAD_DIM

    def run(query, key_in, value_in, out_grad, lengths):
        heads = heads_of(query.shape[1])
        near = max(r for r in range(1, ctx + 1) if ctx % r == 0 and heads % (r * tp) == 0)
        finer = Mesh(mesh.devices.reshape(ctx // near, near, tp), ("g", "r", "tp"))
        placed = P(("g", "r", "tp"), None)
        return jax.shard_map(
            shards,
            mesh=finer,
            in_specs=(placed,) * 4 + (P(),),
            out_specs=(placed,) * 3,
            check_vma=False,
        )(query, key_in, value_in, out_grad, lengths)

    return run
```

```python
import functools

import jax
import jax.numpy as jnp
import numpy as np
from jax import lax
from jax.experimental import pallas as pl
from jax.experimental.pallas import tpu as pltpu
from jax.sharding import Mesh
from jax.sharding import PartitionSpec as P

HEAD_DIM = 128
NEG = -1e30
FLOOR = -1e29
UNIT = 128
CHUNK = 2
TILE = 256
WIDTHS = (4, 5, 6, 8, 10)


def copy_all(pairs, sems):
    copies = [
        pltpu.make_async_copy(source, target, sems.at[number])
        for number, (source, target) in enumerate(pairs)
    ]
    for copy in copies:
        copy.start()
    for copy in copies:
        copy.wait()


def pack_kernel(first, count, *refs):
    ins, (out, sems) = refs[:-2], refs[-2:]
    peers = out.shape[0]
    each = ins[0].shape[1] // peers
    copy_all(
        [
            (ref.at[:, pl.ds(peer * each + first, count)], out.at[peer, kind])
            for peer in range(peers)
            for kind, ref in enumerate(ins)
        ],
        sems,
    )


def pack(arrays, peers, first, count):
    rows = arrays[0].shape[0]
    kinds = len(arrays)
    anywhere = pl.BlockSpec(memory_space=pl.ANY)
    return pl.pallas_call(
        functools.partial(pack_kernel, first, count),
        in_specs=[anywhere] * kinds,
        out_specs=pl.BlockSpec(memory_space=pltpu.VMEM),
        out_shape=jax.ShapeDtypeStruct((peers, kinds, rows, count), arrays[0].dtype),
        scratch_shapes=[pltpu.SemaphoreType.DMA((peers * kinds,))],
        name="pack",
    )(*arrays)


def unpack_kernel(first, kinds, block, *refs):
    outs, sems = refs[-kinds - 1 : -1], refs[-1]
    peers, _, _, count = block.shape
    each = outs[0].shape[1] // peers
    copy_all(
        [
            (block.at[peer, kind], out.at[:, pl.ds(peer * each + first, count)])
            for peer in range(peers)
            for kind, out in enumerate(outs)
        ],
        sems,
    )


def unpack(block, first, width, held):
    peers, kinds, rows, _ = block.shape
    anywhere = pl.BlockSpec(memory_space=pl.ANY)
    return pl.pallas_call(
        functools.partial(unpack_kernel, first, kinds),
        in_specs=[pl.BlockSpec(memory_space=pltpu.VMEM)] + [anywhere] * len(held),
        out_specs=[anywhere] * kinds,
        out_shape=[jax.ShapeDtypeStruct((rows, width), block.dtype)] * kinds,
        input_output_aliases={1 + kind: kind for kind in range(len(held))},
        scratch_shapes=[pltpu.SemaphoreType.DMA((peers * kinds,))],
        name="unpack",
    )(block, *held)


def attention_kernel(
    widths, meta, seg_key, seg_query, left, own, right, out, window, grads_q, dk, dv, sems
):
    heads, kinds, blocks, rows, _ = window.shape
    peers = own.shape[0]
    edge = left.shape[0]
    scale = HEAD_DIM ** (-0.5)
    factor = scale * float(np.log2(np.e))
    unit, tall = UNIT // rows, TILE // rows
    columns = [slice(head * HEAD_DIM, (head + 1) * HEAD_DIM) for head in range(heads)]
    copies = [
        pltpu.make_async_copy(
            source.at[:, kind, :, columns[head]],
            window.at[head, kind, first : first + source.shape[0]],
            sems.at[head, kind, part],
        )
        for head in range(heads)
        for kind in range(kinds)
        for part, (source, first) in enumerate(
            ((left, 0), (own, edge), (right, edge + peers))
        )
    ]
    for copy in copies:
        copy.start()
    dk[...] = jnp.zeros_like(dk)
    dv[...] = jnp.zeros_like(dv)
    for copy in copies:
        copy.wait()

    def flat(value):
        return value.reshape(value.shape[0] * rows, HEAD_DIM)

    def visit(tile, width):
        lanes = pl.ds(pl.multiple_of(tile * TILE, TILE), TILE)
        first = meta[0, tile]
        marks = seg_key[pl.ds(pl.multiple_of(first * UNIT, UNIT), width * UNIT)]
        inside = jnp.concatenate([marks] * (TILE // 128), axis=1) == seg_query[:, lanes]
        here = pl.ds(tile * tall, tall)
        keys = pl.ds(first * unit, width * unit)
        over = (((1,), (1,)), ((), ()))
        query_terms = []
        for head in range(heads):
            q, g = flat(window[head, 0, here]), flat(window[head, 3, here])
            k, v = flat(window[head, 1, keys]), flat(window[head, 2, keys])
            scores = lax.dot_general(k, q, over, preferred_element_type=jnp.float32)
            dprob = lax.dot_general(v, g, over, preferred_element_type=jnp.float32)
            scores = jnp.where(inside, scores, NEG)
            top = jnp.maximum(jnp.max(scores, axis=0, keepdims=True), FLOOR)
            raised = jnp.exp2((scores - top) * factor)
            total = jnp.sum(raised, axis=0, keepdims=True)
            inverse = jnp.where(total > 0.0, 1.0 / total, 0.0)
            dot = jnp.sum(raised * dprob, axis=0, keepdims=True) * inverse
            probs = raised * inverse
            probs_b = probs.astype(jnp.bfloat16)
            dscore = (probs * (dprob - dot)).astype(jnp.bfloat16)
            shape = (width * unit, rows, HEAD_DIM)
            dv[head, keys] += jnp.dot(probs_b, g, preferred_element_type=jnp.float32).reshape(shape)
            dk[head, keys] += jnp.dot(dscore, q, preferred_element_type=jnp.float32).reshape(shape)
            dq = lax.dot_general(
                dscore, k, (((0,), (0,)), ((), ())), preferred_element_type=jnp.float32
            )
            query_terms.append((dq * scale).astype(jnp.bfloat16).reshape(tall, rows, HEAD_DIM))
        for head in range(heads):
            grads_q[head, here] = query_terms[head]

    def step(tile, carry):
        for width in widths:
            pl.when(meta[1, tile] == width)(functools.partial(visit, tile, width))
        return carry

    lax.fori_loop(0, blocks // tall, step, 0)
    for head in range(heads):
        inner = slice(edge, edge + peers)
        out[:, 0, :, columns[head]] = grads_q[head, inner]
        out[:, 1, :, columns[head]] = (dk[head, inner] * scale).astype(jnp.bfloat16)
        out[:, 2, :, columns[head]] = dv[head, inner].astype(jnp.bfloat16)


def attention(meta, seg_key, seg_query, left, own, right, widths):
    peers, kinds, rows, width = own.shape
    blocks = peers + 2 * left.shape[0]
    heads = width // HEAD_DIM
    elements = heads * blocks * rows * 5 * UNIT
    smem = pl.BlockSpec(memory_space=pltpu.SMEM)
    vmem = pl.BlockSpec(memory_space=pltpu.VMEM)
    anywhere = pl.BlockSpec(memory_space=pl.ANY)
    return pl.pallas_call(
        functools.partial(attention_kernel, widths),
        in_specs=[smem, vmem, vmem, anywhere, anywhere, anywhere],
        out_specs=vmem,
        out_shape=jax.ShapeDtypeStruct((peers, 3, rows, width), jnp.bfloat16),
        scratch_shapes=[
            pltpu.VMEM((heads, kinds, blocks, rows, HEAD_DIM), jnp.bfloat16),
            pltpu.VMEM((heads, blocks, rows, HEAD_DIM), jnp.bfloat16),
            pltpu.VMEM((heads, blocks, rows, HEAD_DIM), jnp.float32),
            pltpu.VMEM((heads, blocks, rows, HEAD_DIM), jnp.float32),
            pltpu.SemaphoreType.DMA((heads, kinds, 3)),
        ],
        cost_estimate=pl.CostEstimate(
            flops=elements * 10 * HEAD_DIM,
            transcendentals=elements,
            bytes_accessed=own.size * 4 + left.size * 4,
        ),
        name="attention",
    )(meta, seg_key, seg_query, left, own, right)


def plan(lengths, me, group, halo, tokens, widths):
    window = group + 2 * halo
    count = lengths.shape[0]
    order = jnp.arange(count, dtype=jnp.int32)
    ends = jnp.sum(jnp.where(order[:, None] <= order[None, :], lengths[:, None], 0), axis=0)
    base = me * group - halo
    at = base + jnp.arange(window, dtype=jnp.int32)
    passed = ends[:, None] <= at[None, :]
    seg = jnp.sum(passed.astype(jnp.int32), axis=0)
    start = jnp.sum(jnp.where(passed, lengths[:, None], 0), axis=0)
    end = jnp.min(jnp.where(passed, tokens, ends[:, None]), axis=0)
    touches = (start < (me + 1) * group) & (end > me * group)
    valid = touches & (at >= 0) & (at < tokens)
    seg_key = jnp.broadcast_to(jnp.where(valid, seg, -1)[:, None], (window, 128))
    seg_query = jnp.where(valid, seg, -2)[None, :]
    first = jnp.min(jnp.where(valid, start - base, window).reshape(-1, TILE), axis=1) // UNIT
    last = jnp.max(jnp.where(valid, end - base, 0).reshape(-1, TILE), axis=1)
    need = (last + UNIT - 1) // UNIT - first
    chosen = jnp.full_like(need, widths[-1])
    for width in reversed(widths):
        chosen = jnp.where(need <= width, width, chosen)
    chosen = jnp.where(last > 0, chosen, 0)
    first = jnp.clip(first, 0, window // UNIT - chosen)
    return jnp.stack([first, chosen]).astype(jnp.int32), seg_key, seg_query


def shards(query, key_in, value_in, out_grad, lengths):
    arrays = (query, key_in, value_in, out_grad)
    plane = ("r", "tp")
    groups = lax.axis_size("g")
    peers = lax.axis_size("r") * lax.axis_size("tp")
    rows, width = query.shape
    each = width // peers
    group = rows * peers
    edge = lax.axis_size("tp")
    halo = rows * edge
    window = group + 2 * halo
    tokens = group * groups
    widths = tuple(w for w in WIDTHS if w < window // UNIT and w <= 10)
    if window // UNIT <= 10:
        widths = widths + (window // UNIT,)
    meta, seg_key, seg_query = plan(lengths, lax.axis_index("g"), group, halo, tokens, widths)
    up = [(i, i + 1) for i in range(groups - 1)]
    down = [(i + 1, i) for i in range(groups - 1)]
    heads = each // HEAD_DIM
    spans = [
        (first * HEAD_DIM, min(CHUNK, heads - first) * HEAD_DIM)
        for first in range(0, heads, CHUNK)
    ]

    def exchange(block, after):
        if after is not None:
            block, _ = lax.optimization_barrier((block, after))
        return lax.all_to_all(block, plane, split_axis=0, concat_axis=0, tiled=True)

    last, gathered = None, []
    for first, count in spans:
        packed = pack(arrays, peers, first, count)
        last = exchange(packed, last)
        gathered.append(last)
    outs = []
    for own, (first, count) in zip(gathered, spans):
        left = lax.ppermute(own[peers - edge :], "g", up)
        right = lax.ppermute(own[:edge], "g", down)
        grads = attention(meta, seg_key, seg_query, left, own, right, widths)
        last = exchange(grads, last)
        outs = unpack(last, first, width, outs)
    return tuple(outs)


def solution(mesh):
    ctx, tp = mesh.devices.shape
    heads_of = lambda width: width // HEAD_DIM

    def run(query, key_in, value_in, out_grad, lengths):
        heads = heads_of(query.shape[1])
        near = max(r for r in range(1, ctx + 1) if ctx % r == 0 and heads % (r * tp) == 0)
        finer = Mesh(mesh.devices.reshape(ctx // near, near, tp), ("g", "r", "tp"))
        placed = P(("g", "r", "tp"), None)
        return jax.shard_map(
            shards,
            mesh=finer,
            in_specs=(placed,) * 4 + (P(),),
            out_specs=(placed,) * 3,
            check_vma=False,
        )(query, key_in, value_in, out_grad, lengths)

    return run
```

```python
import functools

import jax
import jax.numpy as jnp
import numpy as np
from jax import lax
from jax.experimental import pallas as pl
from jax.experimental.pallas import tpu as pltpu
from jax.sharding import Mesh
from jax.sharding import PartitionSpec as P

HEAD_DIM = 128
NEG = -1e30
FLOOR = -1e29
UNIT = 128
CHUNK = 2
TILE = 256
STRIDE = 2
WIDTHS = (4, 5, 6, 8, 10)


def copy_all(pairs, sems):
    copies = [
        pltpu.make_async_copy(source, target, sems.at[number])
        for number, (source, target) in enumerate(pairs)
    ]
    for copy in copies:
        copy.start()
    for copy in copies:
        copy.wait()


def pack_kernel(first, count, *refs):
    ins, (out, sems) = refs[:-2], refs[-2:]
    peers = out.shape[0]
    each = ins[0].shape[1] // peers
    copy_all(
        [
            (ref.at[:, pl.ds(peer * each + first, count)], out.at[peer, kind])
            for peer in range(peers)
            for kind, ref in enumerate(ins)
        ],
        sems,
    )


def pack(arrays, peers, first, count):
    rows = arrays[0].shape[0]
    kinds = len(arrays)
    anywhere = pl.BlockSpec(memory_space=pltpu.HBM)
    return pl.pallas_call(
        functools.partial(pack_kernel, first, count),
        in_specs=[anywhere] * kinds,
        out_specs=pl.BlockSpec(memory_space=pltpu.VMEM),
        out_shape=jax.ShapeDtypeStruct((peers, kinds, rows, count), arrays[0].dtype),
        scratch_shapes=[pltpu.SemaphoreType.DMA((peers * kinds,))],
        name="pack",
    )(*arrays)


def unpack_kernel(first, kinds, block, *refs):
    outs, sems = refs[-kinds - 1 : -1], refs[-1]
    peers, _, _, count = block.shape
    each = outs[0].shape[1] // peers
    copy_all(
        [
            (block.at[peer, kind], out.at[:, pl.ds(peer * each + first, count)])
            for peer in range(peers)
            for kind, out in enumerate(outs)
        ],
        sems,
    )


def unpack(block, first, width, held):
    peers, kinds, rows, _ = block.shape
    anywhere = pl.BlockSpec(memory_space=pltpu.HBM)
    return pl.pallas_call(
        functools.partial(unpack_kernel, first, kinds),
        in_specs=[pl.BlockSpec(memory_space=pltpu.VMEM)] + [anywhere] * len(held),
        out_specs=[anywhere] * kinds,
        out_shape=[jax.ShapeDtypeStruct((rows, width), block.dtype)] * kinds,
        input_output_aliases={1 + kind: kind for kind in range(len(held))},
        scratch_shapes=[pltpu.SemaphoreType.DMA((peers * kinds,))],
        compiler_params=pltpu.CompilerParams(vmem_limit_bytes=8 << 20),
        name="unpack",
    )(block, *held)


def attention_kernel(
    widths,
    meta,
    marks_in,
    seg_query,
    left,
    own,
    right,
    result,
    seg_key,
    out,
    window,
    grads_q,
    dk,
    dv,
    sems,
    edge_sems,
):
    heads, kinds, blocks, rows, _ = window.shape
    peers = own.shape[0]
    edge = left.shape[0]
    scale = HEAD_DIM ** (-0.5)
    factor = scale * float(np.log2(np.e))
    unit, tall = UNIT // rows, TILE // rows
    columns = [slice(head * HEAD_DIM, (head + 1) * HEAD_DIM) for head in range(heads)]
    copies = [
        pltpu.make_async_copy(
            source.at[:, kind, :, columns[head]],
            window.at[head, kind, first : first + source.shape[0]],
            sems.at[head, kind, part],
        )
        for head in range(heads)
        for kind in range(kinds)
        for part, (source, first) in enumerate(
            ((left, 0), (own, edge), (right, edge + peers))
        )
    ]
    copies.append(pltpu.make_async_copy(marks_in, seg_key, edge_sems.at[0]))
    for copy in copies:
        copy.start()
    dk[...] = jnp.zeros_like(dk)
    dv[...] = jnp.zeros_like(dv)
    for copy in copies:
        copy.wait()

    def flat(value):
        return value.reshape(value.shape[0] * rows, HEAD_DIM)

    def visit(tile, width):
        lanes = pl.ds(pl.multiple_of(tile * TILE, TILE), TILE)
        first = meta[0, tile]
        marks = seg_key[pl.ds(pl.multiple_of(first * UNIT, UNIT), width * UNIT)]
        inside = jnp.concatenate([marks] * (TILE // 128), axis=1) == seg_query[:, lanes]
        here = pl.ds(tile * tall, tall)
        over = (((1,), (1,)), ((), ()))
        down = (((0,), (0,)), ((), ()))
        pieces = [
            (at, min(STRIDE, width - at)) for at in range(0, width, STRIDE)
        ]

        def span(at, count):
            return pl.ds((first + at) * unit, count * unit)

        def dot(left, right, dims):
            return lax.dot_general(left, right, dims, preferred_element_type=jnp.float32)

        plain = (((1,), (0,)), ((), ()))
        query_terms, held = [], []
        for head in range(heads):
            q = flat(window[head, 0, here])
            scores, top = [], FLOOR
            for at, count in pieces:
                piece = dot(flat(window[head, 1, span(at, count)]), q, over)
                piece = jnp.where(inside[at * UNIT : (at + count) * UNIT], piece, NEG)
                scores.append(piece)
                top = jnp.maximum(top, jnp.max(piece, axis=0, keepdims=True))
            held.append((scores, top))
        middle = []
        for head in range(heads):
            g = flat(window[head, 3, here])
            scores, top = held[head]
            raised, dprobs, total, product = [], [], 0.0, 0.0
            for (at, count), piece in zip(pieces, scores):
                dprob = dot(flat(window[head, 2, span(at, count)]), g, over)
                piece = jnp.exp2((piece - top) * factor)
                total = total + jnp.sum(piece, axis=0, keepdims=True)
                product = product + jnp.sum(piece * dprob, axis=0, keepdims=True)
                raised.append(piece)
                dprobs.append(dprob)
            middle.append((raised, dprobs, total, product))
        for head in range(heads):
            q, g = flat(window[head, 0, here]), flat(window[head, 3, here])
            raised, dprobs, total, product = middle[head]
            inverse = jnp.where(total > 0.0, 1.0 / total, 0.0)
            product = product * inverse
            dq = 0.0
            for (at, count), piece, dprob in zip(pieces, raised, dprobs):
                probs = piece * inverse
                dscore = (probs * (dprob - product)).astype(jnp.bfloat16)
                keys = span(at, count)
                shape = (count * unit, rows, HEAD_DIM)
                dv[head, keys] += dot(probs.astype(jnp.bfloat16), g, plain).reshape(shape)
                dk[head, keys] += dot(dscore, q, plain).reshape(shape)
                dq = dq + dot(dscore, flat(window[head, 1, keys]), down)
            query_terms.append((dq * scale).astype(jnp.bfloat16).reshape(tall, rows, HEAD_DIM))
        for head in range(heads):
            grads_q[head, here] = query_terms[head]

    def step(tile, carry):
        for width in widths:
            pl.when(meta[1, tile] == width)(functools.partial(visit, tile, width))
        return carry

    lax.fori_loop(0, blocks // tall, step, 0)
    for head in range(heads):
        inner = slice(edge, edge + peers)
        out[:, 0, :, columns[head]] = grads_q[head, inner]
        out[:, 1, :, columns[head]] = (dk[head, inner] * scale).astype(jnp.bfloat16)
        out[:, 2, :, columns[head]] = dv[head, inner].astype(jnp.bfloat16)
    leaving = pltpu.make_async_copy(out, result, edge_sems.at[1])
    leaving.start()
    leaving.wait()


def attention(meta, seg_key, seg_query, left, own, right, widths):
    peers, kinds, rows, width = own.shape
    blocks = peers + 2 * left.shape[0]
    heads = width // HEAD_DIM
    elements = heads * blocks * rows * 5 * UNIT
    smem = pl.BlockSpec(memory_space=pltpu.SMEM)
    vmem = pl.BlockSpec(memory_space=pltpu.VMEM)
    outer = pl.BlockSpec(memory_space=pltpu.HBM)
    anywhere = pl.BlockSpec(memory_space=pl.ANY)
    return pl.pallas_call(
        functools.partial(attention_kernel, widths),
        in_specs=[smem, outer, vmem, anywhere, anywhere, anywhere],
        out_specs=outer,
        out_shape=pltpu.HBM((peers, 3, rows, width), jnp.bfloat16),
        scratch_shapes=[
            pltpu.VMEM(seg_key.shape, jnp.int32),
            pltpu.VMEM((peers, 3, rows, width), jnp.bfloat16),
            pltpu.VMEM((heads, kinds, blocks, rows, HEAD_DIM), jnp.bfloat16),
            pltpu.VMEM((heads, blocks, rows, HEAD_DIM), jnp.bfloat16),
            pltpu.VMEM((heads, blocks, rows, HEAD_DIM), jnp.float32),
            pltpu.VMEM((heads, blocks, rows, HEAD_DIM), jnp.float32),
            pltpu.SemaphoreType.DMA((heads, kinds, 3)),
            pltpu.SemaphoreType.DMA((2,)),
        ],
        cost_estimate=pl.CostEstimate(
            flops=elements * 10 * HEAD_DIM,
            transcendentals=elements,
            bytes_accessed=own.size * 4 + left.size * 4,
        ),
        compiler_params=pltpu.CompilerParams(vmem_limit_bytes=32 << 20),
        name="attention",
    )(
        meta,
        pltpu.with_memory_space_constraint(seg_key, pltpu.HBM),
        seg_query,
        left,
        own,
        right,
    )


def plan(lengths, me, group, halo, tokens, widths):
    window = group + 2 * halo
    count = lengths.shape[0]
    order = jnp.arange(count, dtype=jnp.int32)
    ends = jnp.sum(jnp.where(order[:, None] <= order[None, :], lengths[:, None], 0), axis=0)
    base = me * group - halo
    at = base + jnp.arange(window, dtype=jnp.int32)
    passed = ends[:, None] <= at[None, :]
    seg = jnp.sum(passed.astype(jnp.int32), axis=0)
    start = jnp.sum(jnp.where(passed, lengths[:, None], 0), axis=0)
    end = jnp.min(jnp.where(passed, tokens, ends[:, None]), axis=0)
    touches = (start < (me + 1) * group) & (end > me * group)
    valid = touches & (at >= 0) & (at < tokens)
    seg_key = jnp.broadcast_to(jnp.where(valid, seg, -1)[:, None], (window, 128))
    seg_query = jnp.where(valid, seg, -2)[None, :]
    first = jnp.min(jnp.where(valid, start - base, window).reshape(-1, TILE), axis=1) // UNIT
    last = jnp.max(jnp.where(valid, end - base, 0).reshape(-1, TILE), axis=1)
    need = (last + UNIT - 1) // UNIT - first
    chosen = jnp.full_like(need, widths[-1])
    for width in reversed(widths):
        chosen = jnp.where(need <= width, width, chosen)
    chosen = jnp.where(last > 0, chosen, 0)
    first = jnp.clip(first, 0, window // UNIT - chosen)
    return jnp.stack([first, chosen]).astype(jnp.int32), seg_key, seg_query


def shards(query, key_in, value_in, out_grad, lengths):
    arrays = (query, key_in, value_in, out_grad)
    plane = ("r", "tp")
    groups = lax.axis_size("g")
    peers = lax.axis_size("r") * lax.axis_size("tp")
    rows, width = query.shape
    each = width // peers
    group = rows * peers
    edge = lax.axis_size("tp")
    halo = rows * edge
    window = group + 2 * halo
    tokens = group * groups
    widths = tuple(w for w in WIDTHS if w < window // UNIT and w <= 10)
    if window // UNIT <= 10:
        widths = widths + (window // UNIT,)
    meta, seg_key, seg_query = plan(lengths, lax.axis_index("g"), group, halo, tokens, widths)
    up = [(i, i + 1) for i in range(groups - 1)]
    down = [(i + 1, i) for i in range(groups - 1)]
    heads = each // HEAD_DIM
    cuts = [0] + list(range(heads % CHUNK or CHUNK, heads + 1, CHUNK))
    spans = [
        (first * HEAD_DIM, (last - first) * HEAD_DIM) for first, last in zip(cuts, cuts[1:])
    ]

    def exchange(block, after):
        if after is not None:
            block, _ = lax.optimization_barrier((block, after))
        return lax.all_to_all(block, plane, split_axis=0, concat_axis=0, tiled=True)

    last, gathered = None, []
    for first, count in spans:
        packed = pack(arrays, peers, first, count)
        last = exchange(packed, last)
        gathered.append(last)
    outs = []
    for own, (first, count) in zip(gathered, spans):
        left = lax.ppermute(own[peers - edge :], "g", up)
        right = lax.ppermute(own[:edge], "g", down)
        grads = attention(meta, seg_key, seg_query, left, own, right, widths)
        last = exchange(grads, last)
        outs = unpack(last, first, width, outs)
    return tuple(outs)


def solution(mesh):
    ctx, tp = mesh.devices.shape
    heads_of = lambda width: width // HEAD_DIM

    def run(query, key_in, value_in, out_grad, lengths):
        heads = heads_of(query.shape[1])
        near = max(r for r in range(1, ctx + 1) if ctx % r == 0 and heads % (r * tp) == 0)
        finer = Mesh(mesh.devices.reshape(ctx // near, near, tp), ("g", "r", "tp"))
        placed = P(("g", "r", "tp"), None)
        return jax.shard_map(
            shards,
            mesh=finer,
            in_specs=(placed,) * 4 + (P(),),
            out_specs=(placed,) * 3,
            check_vma=False,
        )(query, key_in, value_in, out_grad, lengths)

    return run
```

```python
import functools

import jax
import jax.numpy as jnp
import numpy as np
from jax import lax
from jax.experimental import pallas as pl
from jax.experimental.pallas import tpu as pltpu
from jax.sharding import Mesh
from jax.sharding import PartitionSpec as P

HEAD_DIM = 128
NEG = -1e30
FLOOR = -1e29
UNIT = 128
STEP = 16
CHUNK = 2
TILE = 256
STRIDE = 2
WIDTHS = (3, 4, 5, 6, 8, 10)


def copy_all(pairs, sems):
    copies = [
        pltpu.make_async_copy(source, target, sems.at[number])
        for number, (source, target) in enumerate(pairs)
    ]
    for copy in copies:
        copy.start()
    for copy in copies:
        copy.wait()


def pack_kernel(first, count, *refs):
    ins, (out, sems) = refs[:-2], refs[-2:]
    peers = out.shape[0]
    each = ins[0].shape[1] // peers
    copy_all(
        [
            (ref.at[:, pl.ds(peer * each + first, count)], out.at[peer, kind])
            for peer in range(peers)
            for kind, ref in enumerate(ins)
        ],
        sems,
    )


def pack(arrays, peers, first, count):
    rows = arrays[0].shape[0]
    kinds = len(arrays)
    anywhere = pl.BlockSpec(memory_space=pltpu.HBM)
    return pl.pallas_call(
        functools.partial(pack_kernel, first, count),
        in_specs=[anywhere] * kinds,
        out_specs=pl.BlockSpec(memory_space=pltpu.VMEM),
        out_shape=jax.ShapeDtypeStruct((peers, kinds, rows, count), arrays[0].dtype),
        scratch_shapes=[pltpu.SemaphoreType.DMA((peers * kinds,))],
        name="pack",
    )(*arrays)


def unpack_kernel(first, kinds, block, *refs):
    outs, sems = refs[-kinds - 1 : -1], refs[-1]
    peers, _, _, count = block.shape
    each = outs[0].shape[1] // peers
    copy_all(
        [
            (block.at[peer, kind], out.at[:, pl.ds(peer * each + first, count)])
            for peer in range(peers)
            for kind, out in enumerate(outs)
        ],
        sems,
    )


def unpack(block, first, width, held):
    peers, kinds, rows, _ = block.shape
    anywhere = pl.BlockSpec(memory_space=pltpu.HBM)
    return pl.pallas_call(
        functools.partial(unpack_kernel, first, kinds),
        in_specs=[pl.BlockSpec(memory_space=pltpu.VMEM)] + [anywhere] * len(held),
        out_specs=[anywhere] * kinds,
        out_shape=[jax.ShapeDtypeStruct((rows, width), block.dtype)] * kinds,
        input_output_aliases={1 + kind: kind for kind in range(len(held))},
        scratch_shapes=[pltpu.SemaphoreType.DMA((peers * kinds,))],
        compiler_params=pltpu.CompilerParams(vmem_limit_bytes=8 << 20),
        name="unpack",
    )(block, *held)


def attention_kernel(
    widths,
    meta,
    marks_in,
    seg_query,
    left,
    own,
    right,
    result,
    seg_key,
    out,
    window,
    grads_q,
    dk,
    dv,
    sems,
    edge_sems,
):
    heads, kinds, height, _ = window.shape
    peers, _, rows, _ = own.shape
    edge = left.shape[0]
    scale = HEAD_DIM ** (-0.5)
    factor = scale * float(np.log2(np.e))
    columns = [slice(head * HEAD_DIM, (head + 1) * HEAD_DIM) for head in range(heads)]
    copies = [
        pltpu.make_async_copy(
            source.at[:, kind, :, columns[head]],
            window.at[head, kind]
            .reshape(height // rows, rows, HEAD_DIM)
            .at[first : first + source.shape[0]],
            sems.at[head, kind, part],
        )
        for head in range(heads)
        for kind in range(kinds)
        for part, (source, first) in enumerate(
            ((left, 0), (own, edge), (right, edge + peers))
        )
    ]
    copies.append(pltpu.make_async_copy(marks_in, seg_key, edge_sems.at[0]))
    for copy in copies:
        copy.start()
    inner = slice(edge * rows, (edge + peers) * rows)
    for head in range(heads):
        dk[head, inner] = jnp.zeros((peers * rows, HEAD_DIM), jnp.float32)
        dv[head, inner] = jnp.zeros((peers * rows, HEAD_DIM), jnp.float32)
    for copy in copies:
        copy.wait()

    def visit(tile, width):
        lanes = pl.ds(pl.multiple_of(tile * TILE, TILE), TILE)
        first = meta[0, tile]
        marks = seg_key[pl.ds(pl.multiple_of(first * STEP, STEP), width * UNIT)]
        inside = jnp.concatenate([marks] * (TILE // 128), axis=1) == seg_query[:, lanes]
        here = lanes
        over = (((1,), (1,)), ((), ()))
        down = (((0,), (0,)), ((), ()))
        pieces = [
            (at, min(STRIDE, width - at)) for at in range(0, width, STRIDE)
        ]

        def span(at, count):
            return pl.ds(pl.multiple_of(first * STEP + at * UNIT, STEP), count * UNIT)

        def dot(left, right, dims):
            return lax.dot_general(left, right, dims, preferred_element_type=jnp.float32)

        plain = (((1,), (0,)), ((), ()))
        query_terms, held = [], []
        for head in range(heads):
            q = window[head, 0, here]
            scores, top = [], FLOOR
            for at, count in pieces:
                piece = dot(window[head, 1, span(at, count)], q, over)
                piece = jnp.where(inside[at * UNIT : (at + count) * UNIT], piece, NEG)
                scores.append(piece)
                top = jnp.maximum(top, jnp.max(piece, axis=0, keepdims=True))
            held.append((scores, top))
        middle = []
        for head in range(heads):
            g = window[head, 3, here]
            scores, top = held[head]
            raised, dprobs, total, product = [], [], 0.0, 0.0
            for (at, count), piece in zip(pieces, scores):
                dprob = dot(window[head, 2, span(at, count)], g, over)
                piece = jnp.exp2((piece - top) * factor)
                total = total + jnp.sum(piece, axis=0, keepdims=True)
                product = product + jnp.sum(piece * dprob, axis=0, keepdims=True)
                raised.append(piece)
                dprobs.append(dprob)
            middle.append((raised, dprobs, total, product))
        for head in range(heads):
            q, g = window[head, 0, here], window[head, 3, here]
            raised, dprobs, total, product = middle[head]
            inverse = jnp.where(total > 0.0, 1.0 / total, 0.0)
            product = product * inverse
            dq = 0.0
            for (at, count), piece, dprob in zip(pieces, raised, dprobs):
                probs = piece * inverse
                dscore = (probs * (dprob - product)).astype(jnp.bfloat16)
                keys = span(at, count)
                dv[head, keys] += dot(probs.astype(jnp.bfloat16), g, plain)
                dk[head, keys] += dot(dscore, q, plain)
                dq = dq + dot(dscore, window[head, 1, keys], down)
            query_terms.append((dq * scale).astype(jnp.bfloat16))
        for head in range(heads):
            grads_q[head, here] = query_terms[head]

    def step(tile, carry):
        for width in widths:
            pl.when(meta[1, tile] == width)(functools.partial(visit, tile, width))
        return carry

    lax.fori_loop(0, height // TILE, step, 0)
    for head in range(heads):
        shape = (peers, rows, HEAD_DIM)
        out[:, 0, :, columns[head]] = grads_q[head, inner].reshape(shape)
        out[:, 1, :, columns[head]] = (
            (dk[head, inner] * scale).astype(jnp.bfloat16).reshape(shape)
        )
        out[:, 2, :, columns[head]] = dv[head, inner].astype(jnp.bfloat16).reshape(shape)
    leaving = pltpu.make_async_copy(out, result, edge_sems.at[1])
    leaving.start()
    leaving.wait()


def attention(meta, seg_key, seg_query, left, own, right, widths):
    peers, kinds, rows, width = own.shape
    height = (peers + 2 * left.shape[0]) * rows
    heads = width // HEAD_DIM
    elements = heads * height * 5 * UNIT
    smem = pl.BlockSpec(memory_space=pltpu.SMEM)
    vmem = pl.BlockSpec(memory_space=pltpu.VMEM)
    outer = pl.BlockSpec(memory_space=pltpu.HBM)
    anywhere = pl.BlockSpec(memory_space=pl.ANY)
    return pl.pallas_call(
        functools.partial(attention_kernel, widths),
        in_specs=[smem, outer, vmem, anywhere, anywhere, anywhere],
        out_specs=outer,
        out_shape=pltpu.HBM((peers, 3, rows, width), jnp.bfloat16),
        scratch_shapes=[
            pltpu.VMEM(seg_key.shape, jnp.int32),
            pltpu.VMEM((peers, 3, rows, width), jnp.bfloat16),
            pltpu.VMEM((heads, kinds, height, HEAD_DIM), jnp.bfloat16),
            pltpu.VMEM((heads, height, HEAD_DIM), jnp.bfloat16),
            pltpu.VMEM((heads, height, HEAD_DIM), jnp.float32),
            pltpu.VMEM((heads, height, HEAD_DIM), jnp.float32),
            pltpu.SemaphoreType.DMA((heads, kinds, 3)),
            pltpu.SemaphoreType.DMA((2,)),
        ],
        cost_estimate=pl.CostEstimate(
            flops=elements * 10 * HEAD_DIM,
            transcendentals=elements,
            bytes_accessed=own.size * 4 + left.size * 4,
        ),
        compiler_params=pltpu.CompilerParams(vmem_limit_bytes=32 << 20),
        name="attention",
    )(
        meta,
        pltpu.with_memory_space_constraint(seg_key, pltpu.HBM),
        seg_query,
        left,
        own,
        right,
    )


def plan(lengths, me, group, halo, tokens, widths):
    window = group + 2 * halo
    count = lengths.shape[0]
    order = jnp.arange(count, dtype=jnp.int32)
    ends = jnp.sum(jnp.where(order[:, None] <= order[None, :], lengths[:, None], 0), axis=0)
    base = me * group - halo
    at = base + jnp.arange(window, dtype=jnp.int32)
    passed = ends[:, None] <= at[None, :]
    seg = jnp.sum(passed.astype(jnp.int32), axis=0)
    start = jnp.sum(jnp.where(passed, lengths[:, None], 0), axis=0)
    end = jnp.min(jnp.where(passed, tokens, ends[:, None]), axis=0)
    touches = (start < (me + 1) * group) & (end > me * group)
    valid = touches & (at >= 0) & (at < tokens)
    seg_key = jnp.broadcast_to(jnp.where(valid, seg, -1)[:, None], (window, 128))
    seg_query = jnp.where(valid, seg, -2)[None, :]
    first = jnp.min(jnp.where(valid, start - base, window).reshape(-1, TILE), axis=1) // STEP
    last = jnp.max(jnp.where(valid, end - base, 0).reshape(-1, TILE), axis=1)
    need = (last - first * STEP + UNIT - 1) // UNIT
    chosen = jnp.full_like(need, widths[-1])
    for width in reversed(widths):
        chosen = jnp.where(need <= width, width, chosen)
    chosen = jnp.where(last > 0, chosen, 0)
    first = jnp.clip(first, 0, (window - chosen * UNIT) // STEP)
    return jnp.stack([first, chosen]).astype(jnp.int32), seg_key, seg_query


def shards(query, key_in, value_in, out_grad, lengths):
    arrays = (query, key_in, value_in, out_grad)
    plane = ("r", "tp")
    groups = lax.axis_size("g")
    peers = lax.axis_size("r") * lax.axis_size("tp")
    rows, width = query.shape
    each = width // peers
    group = rows * peers
    edge = lax.axis_size("tp")
    halo = rows * edge
    window = group + 2 * halo
    tokens = group * groups
    widths = tuple(w for w in WIDTHS if w < window // UNIT and w <= 10)
    if window // UNIT <= 10:
        widths = widths + (window // UNIT,)
    meta, seg_key, seg_query = plan(lengths, lax.axis_index("g"), group, halo, tokens, widths)
    up = [(i, i + 1) for i in range(groups - 1)]
    down = [(i + 1, i) for i in range(groups - 1)]
    heads = each // HEAD_DIM
    cuts = [0] + list(range(heads % CHUNK or CHUNK, heads + 1, CHUNK))
    spans = [
        (first * HEAD_DIM, (last - first) * HEAD_DIM) for first, last in zip(cuts, cuts[1:])
    ]

    def exchange(block, after):
        if after is not None:
            block, _ = lax.optimization_barrier((block, after))
        return lax.all_to_all(block, plane, split_axis=0, concat_axis=0, tiled=True)

    last, gathered = None, []
    for first, count in spans:
        packed = pack(arrays, peers, first, count)
        last = exchange(packed, last)
        gathered.append(last)
    outs = []
    for own, (first, count) in zip(gathered, spans):
        left = lax.ppermute(own[peers - edge :], "g", up)
        right = lax.ppermute(own[:edge], "g", down)
        grads = attention(meta, seg_key, seg_query, left, own, right, widths)
        last = exchange(grads, last)
        outs = unpack(last, first, width, outs)
    return tuple(outs)


def solution(mesh):
    ctx, tp = mesh.devices.shape
    heads_of = lambda width: width // HEAD_DIM

    def run(query, key_in, value_in, out_grad, lengths):
        heads = heads_of(query.shape[1])
        near = max(r for r in range(1, ctx + 1) if ctx % r == 0 and heads % (r * tp) == 0)
        finer = Mesh(mesh.devices.reshape(ctx // near, near, tp), ("g", "r", "tp"))
        placed = P(("g", "r", "tp"), None)
        return jax.shard_map(
            shards,
            mesh=finer,
            in_specs=(placed,) * 4 + (P(),),
            out_specs=(placed,) * 3,
            check_vma=False,
        )(query, key_in, value_in, out_grad, lengths)

    return run
```

```python
import functools

import jax
import jax.numpy as jnp
import numpy as np
from jax import lax
from jax.experimental import pallas as pl
from jax.experimental.pallas import tpu as pltpu
from jax.sharding import Mesh
from jax.sharding import PartitionSpec as P

HEAD_DIM = 128
NEG = -1e30
FLOOR = -1e29
UNIT = 128
STEP = 16
CHUNK = 2
TILE = 256
STRIDE = 2
WIDTHS = (3, 4, 5, 6, 8, 10)


def copy_all(pairs, sems):
    copies = [
        pltpu.make_async_copy(source, target, sems.at[number])
        for number, (source, target) in enumerate(pairs)
    ]
    for copy in copies:
        copy.start()
    for copy in copies:
        copy.wait()


def pack_kernel(first, count, *refs):
    ins, (out, block, sems, out_sems) = refs[:-4], refs[-4:]
    peers = out.shape[0]
    each = ins[0].shape[1] // peers
    entering = [
        [
            pltpu.make_async_copy(
                ref.at[:, pl.ds(peer * each + first, count)],
                block.at[peer, kind],
                sems.at[peer, kind],
            )
            for kind, ref in enumerate(ins)
        ]
        for peer in range(peers)
    ]
    leaving = [
        pltpu.make_async_copy(block.at[peer], out.at[peer], out_sems.at[peer])
        for peer in range(peers)
    ]
    for copies in entering:
        for copy in copies:
            copy.start()
    for copies, copy_out in zip(entering, leaving):
        for copy in copies:
            copy.wait()
        copy_out.start()
    for copy_out in leaving:
        copy_out.wait()


def pack(arrays, peers, first, count):
    rows = arrays[0].shape[0]
    kinds = len(arrays)
    shape = (peers, kinds, rows, count)
    anywhere = pl.BlockSpec(memory_space=pltpu.HBM)
    return pl.pallas_call(
        functools.partial(pack_kernel, first, count),
        in_specs=[anywhere] * kinds,
        out_specs=anywhere,
        out_shape=pltpu.HBM(shape, arrays[0].dtype),
        scratch_shapes=[
            pltpu.VMEM(shape, arrays[0].dtype),
            pltpu.SemaphoreType.DMA((peers, kinds)),
            pltpu.SemaphoreType.DMA((peers,)),
        ],
        name="pack",
    )(*arrays)


def unpack_kernel(first, kinds, block, *refs):
    outs, sems = refs[-kinds - 1 : -1], refs[-1]
    peers, _, _, count = block.shape
    each = outs[0].shape[1] // peers
    copy_all(
        [
            (block.at[peer, kind], out.at[:, pl.ds(peer * each + first, count)])
            for peer in range(peers)
            for kind, out in enumerate(outs)
        ],
        sems,
    )


def unpack(block, first, width, held):
    peers, kinds, rows, _ = block.shape
    anywhere = pl.BlockSpec(memory_space=pltpu.HBM)
    return pl.pallas_call(
        functools.partial(unpack_kernel, first, kinds),
        in_specs=[pl.BlockSpec(memory_space=pltpu.VMEM)] + [anywhere] * len(held),
        out_specs=[anywhere] * kinds,
        out_shape=[jax.ShapeDtypeStruct((rows, width), block.dtype)] * kinds,
        input_output_aliases={1 + kind: kind for kind in range(len(held))},
        scratch_shapes=[pltpu.SemaphoreType.DMA((peers * kinds,))],
        compiler_params=pltpu.CompilerParams(vmem_limit_bytes=8 << 20),
        name="unpack",
    )(block, *held)


def attention_kernel(
    widths,
    meta,
    marks_in,
    seg_query,
    left,
    own,
    right,
    result,
    seg_key,
    out,
    window,
    grads_q,
    dk,
    dv,
    sems,
    edge_sems,
):
    heads, kinds, height, _ = window.shape
    peers, _, rows, _ = own.shape
    edge = left.shape[0]
    scale = HEAD_DIM ** (-0.5)
    factor = scale * float(np.log2(np.e))
    columns = [slice(head * HEAD_DIM, (head + 1) * HEAD_DIM) for head in range(heads)]
    copies = [
        pltpu.make_async_copy(
            source.at[:, kind, :, columns[head]],
            window.at[head, kind]
            .reshape(height // rows, rows, HEAD_DIM)
            .at[first : first + source.shape[0]],
            sems.at[head, kind, part],
        )
        for head in range(heads)
        for kind in range(kinds)
        for part, (source, first) in enumerate(
            ((left, 0), (own, edge), (right, edge + peers))
        )
    ]
    copies.append(pltpu.make_async_copy(marks_in, seg_key, edge_sems.at[0]))
    for copy in copies:
        copy.start()
    inner = slice(edge * rows, (edge + peers) * rows)
    for head in range(heads):
        dk[head, inner] = jnp.zeros((peers * rows, HEAD_DIM), jnp.float32)
        dv[head, inner] = jnp.zeros((peers * rows, HEAD_DIM), jnp.float32)
    for copy in copies:
        copy.wait()

    def visit(tile, width):
        lanes = pl.ds(pl.multiple_of(tile * TILE, TILE), TILE)
        first = meta[0, tile]
        marks = seg_key[pl.ds(pl.multiple_of(first * STEP, STEP), width * UNIT)]
        inside = jnp.concatenate([marks] * (TILE // 128), axis=1) == seg_query[:, lanes]
        here = lanes
        over = (((1,), (1,)), ((), ()))
        down = (((0,), (0,)), ((), ()))
        pieces = [
            (at, min(STRIDE, width - at)) for at in range(0, width, STRIDE)
        ]

        def span(at, count):
            return pl.ds(pl.multiple_of(first * STEP + at * UNIT, STEP), count * UNIT)

        def dot(left, right, dims):
            return lax.dot_general(left, right, dims, preferred_element_type=jnp.float32)

        plain = (((1,), (0,)), ((), ()))
        query_terms, held = [], []
        for head in range(heads):
            q = window[head, 0, here]
            scores, top = [], FLOOR
            for at, count in pieces:
                piece = dot(window[head, 1, span(at, count)], q, over)
                piece = jnp.where(inside[at * UNIT : (at + count) * UNIT], piece, NEG)
                scores.append(piece)
                top = jnp.maximum(top, jnp.max(piece, axis=0, keepdims=True))
            held.append((scores, top))
        middle = []
        for head in range(heads):
            g = window[head, 3, here]
            scores, top = held[head]
            raised, dprobs, total, product = [], [], 0.0, 0.0
            for (at, count), piece in zip(pieces, scores):
                dprob = dot(window[head, 2, span(at, count)], g, over)
                piece = jnp.exp2((piece - top) * factor)
                total = total + jnp.sum(piece, axis=0, keepdims=True)
                product = product + jnp.sum(piece * dprob, axis=0, keepdims=True)
                raised.append(piece)
                dprobs.append(dprob)
            middle.append((raised, dprobs, total, product))
        for head in range(heads):
            q, g = window[head, 0, here], window[head, 3, here]
            raised, dprobs, total, product = middle[head]
            inverse = jnp.where(total > 0.0, 1.0 / total, 0.0)
            product = product * inverse
            dq = 0.0
            for (at, count), piece, dprob in zip(pieces, raised, dprobs):
                probs = piece * inverse
                dscore = (probs * (dprob - product)).astype(jnp.bfloat16)
                keys = span(at, count)
                dv[head, keys] += dot(probs.astype(jnp.bfloat16), g, plain)
                dk[head, keys] += dot(dscore, q, plain)
                dq = dq + dot(dscore, window[head, 1, keys], down)
            query_terms.append((dq * scale).astype(jnp.bfloat16))
        for head in range(heads):
            grads_q[head, here] = query_terms[head]

    def step(tile, carry):
        for width in widths:
            pl.when(meta[1, tile] == width)(functools.partial(visit, tile, width))
        return carry

    lax.fori_loop(0, height // TILE, step, 0)
    shape = (peers, rows, HEAD_DIM)
    leaving = []
    for kind, (source, weight) in enumerate(((grads_q, None), (dk, scale), (dv, None))):
        for head in range(heads):
            grads = source[head, inner]
            if weight is not None:
                grads = grads * weight
            out[:, kind, :, columns[head]] = grads.astype(jnp.bfloat16).reshape(shape)
        leaving.append(
            pltpu.make_async_copy(out.at[:, kind], result.at[:, kind], edge_sems.at[1 + kind])
        )
        leaving[-1].start()
    for copy in leaving:
        copy.wait()


def attention(meta, seg_key, seg_query, left, own, right, widths):
    peers, kinds, rows, width = own.shape
    height = (peers + 2 * left.shape[0]) * rows
    heads = width // HEAD_DIM
    elements = heads * height * 5 * UNIT
    smem = pl.BlockSpec(memory_space=pltpu.SMEM)
    vmem = pl.BlockSpec(memory_space=pltpu.VMEM)
    outer = pl.BlockSpec(memory_space=pltpu.HBM)
    anywhere = pl.BlockSpec(memory_space=pl.ANY)
    return pl.pallas_call(
        functools.partial(attention_kernel, widths),
        in_specs=[smem, outer, vmem, anywhere, anywhere, anywhere],
        out_specs=outer,
        out_shape=pltpu.HBM((peers, 3, rows, width), jnp.bfloat16),
        scratch_shapes=[
            pltpu.VMEM(seg_key.shape, jnp.int32),
            pltpu.VMEM((peers, 3, rows, width), jnp.bfloat16),
            pltpu.VMEM((heads, kinds, height, HEAD_DIM), jnp.bfloat16),
            pltpu.VMEM((heads, height, HEAD_DIM), jnp.bfloat16),
            pltpu.VMEM((heads, height, HEAD_DIM), jnp.float32),
            pltpu.VMEM((heads, height, HEAD_DIM), jnp.float32),
            pltpu.SemaphoreType.DMA((heads, kinds, 3)),
            pltpu.SemaphoreType.DMA((4,)),
        ],
        cost_estimate=pl.CostEstimate(
            flops=elements * 10 * HEAD_DIM,
            transcendentals=elements,
            bytes_accessed=own.size * 4 + left.size * 4,
        ),
        compiler_params=pltpu.CompilerParams(vmem_limit_bytes=32 << 20),
        name="attention",
    )(
        meta,
        pltpu.with_memory_space_constraint(seg_key, pltpu.HBM),
        seg_query,
        left,
        own,
        right,
    )


def plan(lengths, me, group, halo, tokens, widths):
    window = group + 2 * halo
    count = lengths.shape[0]
    order = jnp.arange(count, dtype=jnp.int32)
    ends = jnp.sum(jnp.where(order[:, None] <= order[None, :], lengths[:, None], 0), axis=0)
    base = me * group - halo
    at = base + jnp.arange(window, dtype=jnp.int32)
    passed = ends[:, None] <= at[None, :]
    seg = jnp.sum(passed.astype(jnp.int32), axis=0)
    start = jnp.sum(jnp.where(passed, lengths[:, None], 0), axis=0)
    end = jnp.min(jnp.where(passed, tokens, ends[:, None]), axis=0)
    touches = (start < (me + 1) * group) & (end > me * group)
    valid = touches & (at >= 0) & (at < tokens)
    seg_key = jnp.broadcast_to(jnp.where(valid, seg, -1)[:, None], (window, 128))
    seg_query = jnp.where(valid, seg, -2)[None, :]
    first = jnp.min(jnp.where(valid, start - base, window).reshape(-1, TILE), axis=1) // STEP
    last = jnp.max(jnp.where(valid, end - base, 0).reshape(-1, TILE), axis=1)
    need = (last - first * STEP + UNIT - 1) // UNIT
    chosen = jnp.full_like(need, widths[-1])
    for width in reversed(widths):
        chosen = jnp.where(need <= width, width, chosen)
    chosen = jnp.where(last > 0, chosen, 0)
    first = jnp.clip(first, 0, (window - chosen * UNIT) // STEP)
    return jnp.stack([first, chosen]).astype(jnp.int32), seg_key, seg_query


def shards(query, key_in, value_in, out_grad, lengths):
    arrays = (query, key_in, value_in, out_grad)
    plane = ("r", "tp")
    groups = lax.axis_size("g")
    peers = lax.axis_size("r") * lax.axis_size("tp")
    rows, width = query.shape
    each = width // peers
    group = rows * peers
    edge = lax.axis_size("tp")
    halo = rows * edge
    window = group + 2 * halo
    tokens = group * groups
    widths = tuple(w for w in WIDTHS if w < window // UNIT and w <= 10)
    if window // UNIT <= 10:
        widths = widths + (window // UNIT,)
    meta, seg_key, seg_query = plan(lengths, lax.axis_index("g"), group, halo, tokens, widths)
    up = [(i, i + 1) for i in range(groups - 1)]
    down = [(i + 1, i) for i in range(groups - 1)]
    heads = each // HEAD_DIM
    cuts = list(range(0, heads, CHUNK)) + [heads]
    spans = [
        (first * HEAD_DIM, (last - first) * HEAD_DIM) for first, last in zip(cuts, cuts[1:])
    ]

    def exchange(block, after):
        if after is not None:
            block, _ = lax.optimization_barrier((block, after))
        return lax.all_to_all(block, plane, split_axis=0, concat_axis=0, tiled=True)

    last, gathered = None, []
    for first, count in spans:
        packed = pack(arrays, peers, first, count)
        last = exchange(packed, last)
        gathered.append(last)
    outs = []
    for own, (first, count) in zip(gathered, spans):
        left = lax.ppermute(own[peers - edge :], "g", up)
        right = lax.ppermute(own[:edge], "g", down)
        grads = attention(meta, seg_key, seg_query, left, own, right, widths)
        last = exchange(grads, last)
        outs = unpack(last, first, width, outs)
    return tuple(outs)


def solution(mesh):
    ctx, tp = mesh.devices.shape
    heads_of = lambda width: width // HEAD_DIM

    def run(query, key_in, value_in, out_grad, lengths):
        heads = heads_of(query.shape[1])
        near = max(r for r in range(1, ctx + 1) if ctx % r == 0 and heads % (r * tp) == 0)
        finer = Mesh(mesh.devices.reshape(ctx // near, near, tp), ("g", "r", "tp"))
        placed = P(("g", "r", "tp"), None)
        return jax.shard_map(
            shards,
            mesh=finer,
            in_specs=(placed,) * 4 + (P(),),
            out_specs=(placed,) * 3,
            check_vma=False,
        )(query, key_in, value_in, out_grad, lengths)

    return run
```
